32 devices in a mesh: groups: 2 (over y), blk: 4 (over z), probe: 2 (over x), sub: 2 (over core).
Axes of the slice: x: 2, y: 2, z: 4, core: 2. Of those that a mesh axis runs over, the one named last changes fastest.
Arguments:
- coords: float32 [3, 16384], P(None, ('groups', 'blk')), parts along dimension 1, may hold values from -4 to 4
- noise_var: float32 [16384], P(('groups', 'blk')), parts along dimension 0, may hold values from 0.5 to 2
- probe_signs: int32 [64, 16384], P('probe', ('groups', 'blk')), parts along dimension 1, may hold values from -1 to 1, as said below
- tile_rows: int32 [8, 2, 96], P(('groups', 'blk'), 'sub'), parts along dimension 0, may hold values from 0 to 15
- tile_cols: int32 [8, 2, 96], P(('groups', 'blk'), 'sub'), parts along dimension 0, may hold values from 0 to 31, as said below
- tile_count: int32 [8, 2], P(('groups', 'blk'), 'sub'), parts along dimension 0, may hold values from 24 to 96
Outputs:
- alphas: float32 [3, 128], P(None, ('groups', 'probe')), parts along dimension 1
- betas: float32 [3, 128], P(None, ('groups', 'probe')), parts along dimension 1
- last_basis: float32 [64, 16384], P('probe', ('groups', 'blk')), parts along dimension 1
- coord_grad: float32 [3, 16384], P(None, ('groups', 'blk')), parts along dimension 1
The draws below stay inside these ranges and needn't reach their ends.
There are 2 independent parts, one for each index of `groups`. The reference program is written for one: setup_inputs(seed, part) draws one part's arguments, and reference() takes and returns one part's arrays. A program takes and returns all parts, laid end to end along the dimension named above; each array names one. Nothing has to cross between parts.
Inputs may be any that keep to these rules, and one draw needn't show every extreme that they name: `probe_signs`: every entry is -1 or 1. tile_cols minus tile_rows lies between 0 and 16 in every slot.
All inputs are finite; a program needn't handle non-finite values.
Results may differ from the reference program's by a relative error of at most 0.00025.
Values sent between devices are 32-bit elements; how exact they have to be, the bound alone decides.
A program may use at most 64 MiB of HBM per device.

```python
import math
import jax
import jax.numpy as jnp
from jax import lax

DIM = 3
BLOCK = 128
PROBES = 64
ITERS = 3
SB = 16
TILES_DEV = 96
NPTS = 8192
N_BLK = 4
N_SUB = 2


def tile_lists(key):
    rows = jax.random.randint(jax.random.fold_in(key, 11), (N_BLK, N_SUB, TILES_DEV), 0, SB)
    offsets = jax.random.randint(jax.random.fold_in(key, 12), (N_BLK, N_SUB, TILES_DEV), 0, SB + 1)
    rows = rows.at[:, :, 0].set(SB - 1).at[:, :, 1].set(0)
    offsets = offsets.at[:, :, 0].set(SB).at[:, :, 1].set(0)
    return (rows.astype(jnp.int32), (rows + offsets).astype(jnp.int32))


def draw_tile_rows(key, part):
    return tile_lists(key)[0]


def draw_tile_cols(key, part):
    return tile_lists(key)[1]


def draw_tile_count(key, part):
    lowest = TILES_DEV // 4
    spread = jax.random.randint(jax.random.fold_in(key, 13), (N_BLK * N_SUB,), 0, 64)
    counts = lowest + (TILES_DEV - lowest) * spread * spread // 3969
    fullest = jax.random.randint(jax.random.fold_in(key, 14), (), 0, N_BLK * N_SUB)
    counts = counts.at[fullest].set(TILES_DEV)
    return counts.reshape(N_BLK, N_SUB).astype(jnp.int32)


def draw_probe_signs(key, part):
    return (2 * jax.random.randint(jax.random.fold_in(key, 15), (PROBES, NPTS), 0, 2) - 1).astype(jnp.int32)


def shard_levels(stream_key, dims, pieces, smallest, top_value):
    def one(dim, blocks):
        draws = jax.random.uniform(jax.random.fold_in(jax.random.fold_in(stream_key, 6), dim), (blocks,), jnp.float32, smallest / len(pieces), top_value / len(pieces))
        return jnp.repeat(jnp.exp(draws), dims[dim] // blocks).reshape((-1,) + (1,) * (len(dims) - dim - 1))

    level = one(*pieces[0])
    for cut in pieces[1:]:
        level = level * one(*cut)
    return level


def bell_draw(rng, extent, scale, limit, pieces=(), held_as=jnp.bfloat16):
    values = jax.random.normal(rng, extent, jnp.float32) * scale
    if len(pieces) > 0:
        values = shard_levels(rng, extent, pieces, -0.22, 0.18) * values
    return jnp.clip(values, min=-limit, max=limit).astype(held_as)


def setup_inputs(seed: int = 0, part: int = 0) -> dict:
    key_list = jax.random.split(jax.random.key(seed), 7)
    part_splits = jax.random.split(jax.random.fold_in(key_list[6], part), 7)
    return {
        "coords": bell_draw(part_splits[0], (DIM, NPTS), 0.7, 4.0, ((1, 4),), jnp.float32),
        "noise_var": jnp.clip(jnp.exp(math.log(2.0) - 1.3862944 * jax.random.uniform(part_splits[1], (NPTS,), jnp.float32) ** shard_levels(part_splits[1], (NPTS,), ((0, 4),), -0.2, 0.2)), 0.5, 2.0),
        "probe_signs": draw_probe_signs(jax.random.fold_in(jax.random.fold_in(key_list[6], part), 71), part),
        "tile_rows": draw_tile_rows(jax.random.fold_in(jax.random.fold_in(key_list[6], part), 71), part),
        "tile_cols": draw_tile_cols(jax.random.fold_in(jax.random.fold_in(key_list[6], part), 71), part),
        "tile_count": draw_tile_count(jax.random.fold_in(jax.random.fold_in(key_list[6], part), 71), part),
    }


SIGNAL_VAR = 0.1
LENGTH_SQ = 2.0
TAPER_SQ = 16.0
WARP_GAIN = 0.4
EPSILON = 1e-06

def tile_kernel(row_pts, col_pts):
    row_warp = row_pts + WARP_GAIN * jnp.tanh(row_pts)
    col_warp = col_pts + WARP_GAIN * jnp.tanh(col_pts)
    dist = jnp.zeros((row_pts.shape[0], row_pts.shape[2], col_pts.shape[2]), row_pts.dtype)
    for coord in range(row_pts.shape[1]):
        differ = row_warp[:, coord, :, None] - col_warp[:, coord, None, :]
        dist = dist + differ * differ
    taper = jnp.maximum(1.0 - dist / TAPER_SQ, 0.0)
    return SIGNAL_VAR * jnp.exp(-dist / (2.0 * LENGTH_SQ)) * taper * taper

def reference(coords, noise_var, probe_signs, tile_rows, tile_cols, tile_count):
    nblocks = SB * N_BLK
    hi = lax.Precision.HIGHEST
    slab = jnp.arange(N_BLK, dtype=jnp.int32)[:, None, None]
    grow = (slab * SB + tile_rows).astype(jnp.int32).reshape(-1, 16)
    gcol = ((slab * SB + tile_cols) % nblocks).astype(jnp.int32).reshape(-1, 16)
    live = jnp.arange(TILES_DEV, dtype=jnp.int32)[None, None, :] < tile_count[:, :, None]
    live = live.astype(coords.dtype).reshape(-1, 16)

    def pts_of(cds, idx):
        blocks = cds.reshape(DIM, nblocks, BLOCK)
        return jnp.transpose(blocks[:, idx, :], (1, 0, 2))

    def apply(vecs):
        vblk = vecs.reshape(PROBES, nblocks, BLOCK)

        def step(acc, item):
            rws, cls, lv = item
            kern = tile_kernel(pts_of(coords, rws), pts_of(coords, cls)) * lv[:, None, None]
            out_row = jnp.einsum('bij,pbj->pbi', kern, vblk[:, cls, :], precision=hi)
            out_col = jnp.einsum('bij,pbi->pbj', kern, vblk[:, rws, :], precision=hi)
            return (acc.at[:, rws, :].add(out_row).at[:, cls, :].add(out_col), None)
        acc, _ = lax.scan(step, jnp.zeros_like(vblk), (grow, gcol, live))
        return acc.reshape(PROBES, -1) + noise_var[None, :] * vecs
    first = probe_signs.astype(coords.dtype)
    current = first
    previous = jnp.zeros_like(first)
    beta = jnp.zeros((PROBES, 1), coords.dtype)
    alpha_list = []
    beta_list = []
    for step_no in range(ITERS):
        work = apply(current) - beta * previous
        alpha = lax.optimization_barrier(jnp.sum(current * work, axis=1)) / NPTS
        work = work - alpha[:, None] * current
        beta = jnp.sqrt(lax.optimization_barrier(jnp.sum(work * work, axis=1)) / NPTS + EPSILON)[:, None]
        previous, current = (current, work / beta)
        alpha_list.append(alpha)
        beta_list.append(beta[:, 0])
    ublk = current.reshape(PROBES, nblocks, BLOCK)
    vblk = first.reshape(PROBES, nblocks, BLOCK)

    def form(cds):

        def step(total, item):
            rws, cls, lv = item
            kern = tile_kernel(pts_of(cds, rws), pts_of(cds, cls)) * lv[:, None, None]
            weight = jnp.einsum('pbi,pbj->bij', ublk[:, rws, :], vblk[:, cls, :], precision=hi)
            weight = weight + jnp.einsum('pbi,pbj->bij', vblk[:, rws, :], ublk[:, cls, :], precision=hi)
            return (total + jnp.sum(kern * weight) / PROBES, None)
        total, _ = lax.scan(jax.checkpoint(step), jnp.zeros((), cds.dtype), (grow, gcol, live))
        return total
    coord_grad = jax.grad(form)(coords)
    return (jnp.stack(alpha_list), jnp.stack(beta_list), current, coord_grad)
```

```python
import functools
import math

import jax
import jax.numpy as jnp
from jax import lax
from jax.experimental import pallas as pl
from jax.experimental.pallas import tpu as pltpu
from jax.sharding import PartitionSpec as P

ITERS = 3
SIGNAL_VAR = 0.1
LENGTH_SQ = 2.0
TAPER_SQ = 16.0
WARP_GAIN = 0.4
EPSILON = 1e-06

F32 = jnp.float32
BF16 = jnp.bfloat16
BL = 128
SB = 16
HB = 8
WB = 5 * HB
OFFS = 2 * SB + 1
PAIRS = HB * (SB + 1)
UNROLL = 4
TINY = 1e-30
SCALE = math.sqrt(TAPER_SQ)
EXPO = -TAPER_SQ / (2.0 * LENGTH_SQ) / math.log(2.0)
SLOPE = TAPER_SQ / (2.0 * LENGTH_SQ)
BUILD_VMEM = 2**22
APPLY_VMEM = 4 * 2**20
GRAD_VMEM = 6 * 2**20
VMEM = pl.BlockSpec(memory_space=pltpu.VMEM)
SMEM = pl.BlockSpec(memory_space=pltpu.SMEM)
HBM = pl.BlockSpec(memory_space=pltpu.HBM)
MESH = pl.DeviceIdType.MESH


def sds(shape, dtype=F32):
    return jax.ShapeDtypeStruct(shape, dtype)


def peer_of(me, step, n, axis):
    to = lax.rem(me + step + n, n)
    return {axis: to // 2, "sub": lax.rem(to, 2)}


def greet(peers):
    barrier = pltpu.get_barrier_semaphore()
    for peer in peers:
        pl.semaphore_signal(barrier, inc=1, device_id=peer, device_id_type=MESH)
    return barrier


def remote(src, dst, send, recv, peer):
    return pltpu.make_async_remote_copy(
        src_ref=src, dst_ref=dst, send_sem=send, recv_sem=recv,
        device_id=peer, device_id_type=MESH,
    )


def ship(own_ref, win_ref, sems, up, down, twin):
    wsend, wrecv, fsend, frecv = sems
    half = lax.axis_index("sub")
    chunks = own_ref.shape[0] // 8
    rows = [pl.ds(8 * c, 8) for c in range(chunks)]
    outs = []
    for c in range(chunks):
        outs.append(remote(own_ref.at[rows[c]], win_ref.at[0, rows[c]], wsend.at[0, c], wrecv.at[0, c], up))
        outs.append(remote(own_ref.at[rows[c]], win_ref.at[4, rows[c]], wsend.at[1, c], wrecv.at[1, c], down))
    for copy in outs:
        copy.start()
    own = remote(own_ref, win_ref.at[1 + 2 * half], fsend.at[chunks], frecv.at[chunks], twin)
    own.start()

    def finish():
        hand = []
        for c in range(chunks):
            piece = win_ref.at[4 - 4 * half, rows[c]]
            remote(piece, piece, wsend.at[0, c], wrecv.at[1 - half, c], twin).wait_recv()
            copy = remote(piece, win_ref.at[3 - 2 * half, rows[c]], fsend.at[c], frecv.at[c], twin)
            copy.start()
            hand.append(copy)
        own.wait()
        for copy in outs:
            copy.wait_send()
        for c in range(chunks):
            other = win_ref.at[4 * half, rows[c]]
            remote(other, other, wsend.at[0, c], wrecv.at[half, c], twin).wait_recv()
        for copy in hand:
            copy.wait()

    return finish


def ship_sems(own):
    chunks = own.shape[0] // 8
    dma = pltpu.SemaphoreType.DMA
    return [dma((2, chunks)), dma((2, chunks)), dma((chunks + 1,)), dma((chunks + 1,))]


def entry_kernel(n, x_ref, r_ref, c_ref, t_ref, win_ref, rows_ref, cols_ref, tots_ref, send, recv, lsem):
    blk, half = lax.axis_index("blk"), lax.axis_index("sub")
    above, below = lax.rem(blk + 1, n), lax.rem(blk + n - 1, n)
    up = {"blk": above, "sub": half}
    down = {"blk": below, "sub": half}
    cross = {"blk": above, "sub": 1 - half}
    under = {"blk": below, "sub": 1 - half}
    twin = {"blk": blk, "sub": 1 - half}
    barrier = greet((up, down, cross, under, twin))
    lists = ((r_ref, rows_ref), (c_ref, cols_ref), (t_ref, tots_ref))
    local = [pltpu.make_async_copy(x_ref, win_ref.at[1], lsem.at[0])]
    for k, (src, dst) in enumerate(lists):
        local.append(pltpu.make_async_copy(src, dst.at[2], lsem.at[1 + k]))
    for copy in local:
        copy.start()
    pl.semaphore_wait(barrier, 5)
    copies = [
        remote(x_ref, win_ref.at[0], send.at[0], recv.at[0], up),
        remote(x_ref, win_ref.at[2], send.at[1], recv.at[1], down),
    ]
    for k, (src, dst) in enumerate(lists):
        for j, (slot, peer) in enumerate(((1, cross), (0, up), (3, twin))):
            at = 2 + 3 * k + j
            copies.append(remote(src, dst.at[slot], send.at[at], recv.at[at], peer))
    for copy in copies:
        copy.start()
    for copy in local:
        copy.wait()
    for copy in copies:
        copy.wait()


def entry(coords, rows, cols, tots):
    dma = pltpu.SemaphoreType.DMA
    return pl.pallas_call(
        functools.partial(entry_kernel, lax.axis_size("blk")),
        out_shape=(
            sds((3,) + coords.shape),
            sds((4,) + rows.shape, jnp.int32),
            sds((4,) + cols.shape, jnp.int32),
            sds((4,) + tots.shape, jnp.int32),
        ),
        in_specs=[VMEM] * 4,
        out_specs=(VMEM,) * 4,
        scratch_shapes=[dma((11,)), dma((11,)), dma((4,))],
        compiler_params=pltpu.CompilerParams(
            collective_id=0, has_side_effects=True, vmem_limit_bytes=2**21
        ),
        name="entry",
    )(coords, rows, cols, tots)


def exchange_kernel(n, own_ref, stat_ref, win_ref, all_ref, *sems):
    *wsems, ssend, srecv, lsem = sems
    half = lax.axis_index("sub")
    me = lax.axis_index("blk") * 2 + half
    twin = {"blk": lax.axis_index("blk"), "sub": 1 - half}
    up, down = peer_of(me, 2, n, "blk"), peer_of(me, -2, n, "blk")
    barrier = greet([peer_of(me, step, n, "blk") for step in range(1, n)])
    local = pltpu.make_async_copy(own_ref, win_ref.at[2], lsem)
    local.start()
    all_ref[me] = stat_ref[...]
    pl.semaphore_wait(barrier, n - 1)
    finish = ship(own_ref, win_ref, wsems, up, down, twin)
    stats = [
        remote(stat_ref, all_ref.at[me], ssend.at[step], srecv.at[step], peer_of(me, step, n, "blk"))
        for step in range(1, n)
    ]
    for copy in stats:
        copy.start()
    local.wait()
    finish()
    for copy in stats:
        copy.wait()


def exchange(own, stat, ident):
    n = lax.axis_size("blk") * 2
    dma = pltpu.SemaphoreType.DMA
    return pl.pallas_call(
        functools.partial(exchange_kernel, n),
        out_shape=(sds((5,) + own.shape), sds((n,) + stat.shape)),
        in_specs=[VMEM, VMEM],
        out_specs=(VMEM, VMEM),
        scratch_shapes=ship_sems(own) + [dma((n,)), dma((n,)), dma],
        compiler_params=pltpu.CompilerParams(
            collective_id=ident, has_side_effects=True, vmem_limit_bytes=2**22
        ),
        name=f"exchange{ident}",
    )(own, stat)


def share_kernel(n, own_ref, all_ref, send, recv, lsem):
    me = lax.axis_index("probe") * 2 + lax.axis_index("sub")

    def device(step):
        to = lax.rem(me + step, n)
        return {"probe": to // 2, "sub": lax.rem(to, 2)}

    barrier = pltpu.get_barrier_semaphore()
    for step in range(1, n):
        pl.semaphore_signal(barrier, inc=1, device_id=device(step), device_id_type=MESH)
    local = pltpu.make_async_copy(own_ref, all_ref.at[me], lsem)
    local.start()
    pl.semaphore_wait(barrier, n - 1)
    copies = []
    for step in range(1, n):
        copies.append(
            pltpu.make_async_remote_copy(
                src_ref=own_ref,
                dst_ref=all_ref.at[me],
                send_sem=send.at[step],
                recv_sem=recv.at[step],
                device_id=device(step),
                device_id_type=MESH,
            )
        )
    for copy in copies:
        copy.start()
    local.wait()
    for copy in copies:
        copy.wait()


def share(own, ident):
    n = lax.axis_size("probe") * 2
    return pl.pallas_call(
        functools.partial(share_kernel, n),
        out_shape=sds((n,) + own.shape),
        in_specs=[VMEM],
        out_specs=VMEM,
        scratch_shapes=[
            pltpu.SemaphoreType.DMA((n,)),
            pltpu.SemaphoreType.DMA((n,)),
            pltpu.SemaphoreType.DMA,
        ],
        compiler_params=pltpu.CompilerParams(collective_id=ident, has_side_effects=True, vmem_limit_bytes=2**21),
        name="share",
    )(own)


def block_of(ref, block, lo, hi):
    return ref[block // HB, lo:hi, (block % HB) * BL : (block % HB + 1) * BL]


def spread_points(x_ref, xb, half):
    for c in range(WB):
        at = c + HB * half
        flat = x_ref[at // SB, :, pl.ds(pl.multiple_of((at % SB) * BL, BL), BL)]
        cols = jnp.concatenate([flat, flat, flat[0:2]], axis=0).T
        for k in range(3):
            xb[c, k] = jnp.broadcast_to(cols[:, k : k + 1], (BL, BL))


def own_row(x_ref, half, a, k):
    return x_ref[1, k : k + 1, pl.ds(pl.multiple_of((a + HB * half) * BL, BL), BL)]


def local_stats(q, w, st_ref):
    square = jnp.sum(q * q, axis=1, keepdims=True)
    guess = jnp.sum(q * w, axis=1, keepdims=True) / jnp.maximum(square, TINY)
    rest = w - guess * q
    resid = jnp.sum(rest * rest, axis=1, keepdims=True)
    lane = lax.broadcasted_iota(jnp.int32, (q.shape[0], BL), 1)
    mixed = jnp.where(lane == 0, guess, jnp.where(lane == 1, resid, square))
    full = jnp.concatenate([mixed] * (BL // q.shape[0]), axis=0)
    st_ref[...] = full.T[0:8, :]


def alpha_beta(st_ref, ab_ref, n, probes, total_pts):
    guess = [st_ref[d, 0:1, :] for d in range(n)]
    square = [st_ref[d, 2:3, :] for d in range(n)]
    alpha = guess[0] * square[0]
    for d in range(1, n):
        alpha = alpha + guess[d] * square[d]
    alpha = alpha / total_pts
    resid = jnp.zeros_like(alpha)
    for d in range(n):
        gap = alpha - guess[d]
        resid = resid + (st_ref[d, 1:2, :] + gap * gap * square[d])
    beta = jnp.sqrt(resid / total_pts + EPSILON)
    row = lax.broadcasted_iota(jnp.int32, (8, BL), 0)
    ab = jnp.where(row == 0, alpha, beta)
    ab_ref[...] = ab
    cols = jnp.concatenate([ab] * 16, axis=0).T
    return cols[0:probes, 0:1], cols[0:probes, 1:2]


def split(value):
    high = value.astype(BF16)
    return high, (value - high.astype(F32)).astype(BF16)


def build_kernel(m_ref, raw_ref, wb_ref, ap_ref, np_ref, k_ref, dbuf, xb, x_ref, mult):
    half = lax.axis_index("sub")
    for slab in range(3):
        raw = raw_ref[slab]
        x_ref[slab] = (raw + WARP_GAIN * jnp.tanh(raw)) * (1.0 / SCALE)

    def fill(a, slot):
        at = slot
        for o in range(OFFS):
            times = m_ref[a * OFFS + o]
            wb_ref[at] = a + o
            mult[at] = times.astype(F32) * SIGNAL_VAR
            ap_ref[at // 2] = a
            at = at + (times > 0).astype(jnp.int32)
        wb_ref[at] = a + SB
        mult[at] = jnp.float32(0.0)
        ap_ref[at // 2] = a
        return slot + (at - slot + 1) // 2 * 2

    slots = lax.fori_loop(0, HB, fill, 0)
    used = slots // 2
    padded = (used + UNROLL - 1) // UNROLL * UNROLL

    def pad(i, _):
        ap_ref[i] = HB - 1
        for e in range(2):
            wb_ref[2 * i + e] = HB - 1 + SB
            mult[2 * i + e] = jnp.float32(0.0)
        return 0

    lax.fori_loop(used, padded, pad, 0)
    np_ref[0] = padded
    spread_points(x_ref, xb, half)

    def step(i, _):
        a = ap_ref[i]
        for e in range(2):
            c = wb_ref[2 * i + e]
            dist = None
            for k in range(3):
                differ = xb[c, k] - own_row(x_ref, half, a, k)
                dist = differ * differ if dist is None else dist + differ * differ
            taper = jnp.maximum(1.0 - dist, 0.0)
            weight = mult[2 * i + e] * jnp.exp2(dist * EXPO) * taper
            high, low = split(weight * taper)
            rows = pl.ds(e * BL, BL)
            k_ref[i, rows, 0:BL] = high
            k_ref[i, rows, BL : 2 * BL] = low
            dbuf[i, rows, :] = weight * (taper * SLOPE + 2.0)
        return 0

    lax.fori_loop(0, padded, step, 0)


def build(m, points):
    return pl.pallas_call(
        build_kernel,
        out_shape=(
            sds((2 * PAIRS + 8,), jnp.int32),
            sds((PAIRS + 8,), jnp.int32),
            sds((1,), jnp.int32),
            pltpu.VMEM((PAIRS, 2 * BL, 2 * BL), BF16),
            pltpu.VMEM((PAIRS, 2 * BL, BL), F32),
            pltpu.VMEM((WB, 3, BL, BL), F32),
            sds(points.shape),
        ),
        in_specs=[SMEM, VMEM],
        out_specs=(SMEM, SMEM, SMEM, VMEM, VMEM, VMEM, VMEM),
        scratch_shapes=[pltpu.SMEM((2 * PAIRS + 8,), F32)],
        compiler_params=pltpu.CompilerParams(vmem_limit_bytes=BUILD_VMEM),
        cost_estimate=pl.CostEstimate(flops=10**9, bytes_accessed=10**7, transcendentals=10**7),
        name="build",
    )(m, points)


def product(wb_ref, ap_ref, count, k_ref, vb, acc, probes):
    acc[...] = jnp.zeros_like(acc)

    def step(u, _):
        made = []
        for t in range(UNROLL):
            i = u * UNROLL + t
            left = jnp.concatenate([vb[wb_ref[2 * i]], vb[wb_ref[2 * i + 1]]], axis=1)
            both = jnp.dot(left, k_ref[i], preferred_element_type=F32)
            both = both[:, 0:BL] + both[:, BL : 2 * BL]
            if both.shape[0] > probes:
                both = both[0:probes] + both[probes:]
            made.append(both)
        for t in range(UNROLL):
            acc[ap_ref[u * UNROLL + t]] += made[t]
        return 0

    lax.fori_loop(0, count // UNROLL, step, 0)


def noise_row(noise_ref, a):
    at = (a + HB * lax.axis_index("sub")) * BL
    return noise_ref[0:1, pl.ds(pl.multiple_of(at, BL), BL)]


def first_kernel(
    wb_ref, ap_ref, np_ref, k_ref, own_ref, below_ref, above_ref, cross_ref, noise_ref, slopes_ref,
    w_ref, st_ref, q_ref, vb, acc,
):
    probes = w_ref.shape[0]
    half = lax.axis_index("sub")

    def place(part, values):
        q_ref[part] = values
        for c in range(HB):
            vb[part * HB + c] = values[:, c * BL : (c + 1) * BL].astype(BF16)

    def own(side):
        at = pl.multiple_of(side * HB * BL, HB * BL)
        return own_ref[:, pl.ds(at, HB * BL)].astype(F32)

    place(0, below_ref[...].astype(F32))
    place(2, own(half))
    place(4, above_ref[...].astype(F32))
    place(1 + 2 * half, cross_ref[...].astype(F32))
    place(3 - 2 * half, own(1 - half))
    product(wb_ref, ap_ref, np_ref[0], k_ref, vb, acc, probes)
    for a in range(HB):
        lanes = slice(a * BL, (a + 1) * BL)
        w_ref[:, lanes] = acc[a] + noise_row(noise_ref, a) * q_ref[2, :, lanes]
    local_stats(q_ref[2], w_ref[...], st_ref)


def first_apply(lists, tiles, slopes, own, below, above, cross, noise):
    probes = own.shape[0]
    return pl.pallas_call(
        first_kernel,
        out_shape=(sds((probes, HB * BL)), sds((8, BL)), sds((5, probes, HB * BL))),
        in_specs=[SMEM, SMEM, SMEM] + [VMEM] * 7,
        out_specs=(VMEM,) * 3,
        scratch_shapes=[
            pltpu.VMEM((WB, probes, BL), BF16),
            pltpu.VMEM((HB, probes, BL), F32),
        ],
        compiler_params=pltpu.CompilerParams(vmem_limit_bytes=APPLY_VMEM),
        name="first_apply",
    )(*lists, tiles, own, below, above, cross, noise, slopes)


def apply_kernel(
    total_pts, wb_ref, ap_ref, np_ref, k_ref, win_ref, old_ref, stat_ref, noise_ref, slopes_ref,
    w_ref, st_ref, q_ref, ab_ref, vb, acc,
):
    probes = win_ref.shape[1]
    alpha, beta = alpha_beta(stat_ref, ab_ref, stat_ref.shape[0], probes, total_pts)
    scale = 1.0 / beta
    for c in range(WB):
        q = (block_of(win_ref, c, 0, probes) - alpha * block_of(old_ref, c, 0, probes)) * scale
        q_ref[c // HB, :, (c % HB) * BL : (c % HB + 1) * BL] = q
        high, low = split(q)
        vb[c, 0:probes, :] = high
        vb[c, probes : 2 * probes, :] = low
    product(wb_ref, ap_ref, np_ref[0], k_ref, vb, acc, probes)
    for a in range(HB):
        lanes = slice(a * BL, (a + 1) * BL)
        w_ref[:, lanes] = (
            acc[a] + noise_row(noise_ref, a) * q_ref[2, :, lanes] - beta * old_ref[2, :, lanes]
        )
    local_stats(q_ref[2], w_ref[...], st_ref)


def apply(lists, tiles, slopes, window, old, stats, noise, total_pts):
    probes = window.shape[1]
    return pl.pallas_call(
        functools.partial(apply_kernel, total_pts),
        out_shape=(
            sds((probes, HB * BL)),
            sds((8, BL)),
            sds((5, probes, HB * BL)),
            sds((8, BL)),
        ),
        in_specs=[SMEM, SMEM, SMEM] + [VMEM] * 6,
        out_specs=(VMEM,) * 4,
        scratch_shapes=[
            pltpu.VMEM((WB, 2 * probes, BL), BF16),
            pltpu.VMEM((HB, probes, BL), F32),
        ],
        compiler_params=pltpu.CompilerParams(vmem_limit_bytes=APPLY_VMEM),
        name="apply",
    )(*lists, tiles, window, old, stats, noise, slopes)


def grad_kernel(
    total_pts, wb_ref, ap_ref, np_ref, dbuf, win_ref, old_ref, stat_ref, first_ref, x_ref, xb,
    ab0, ab1, last_ref, alphas_ref, betas_ref, g_ref, ab2, left_of, right_of, acc,
):
    half = lax.axis_index("sub")
    probes = win_ref.shape[1]

    alpha, beta = alpha_beta(stat_ref, ab2, stat_ref.shape[0], probes, total_pts)
    for it, ab in enumerate((ab0, ab1, ab2)):
        alphas_ref[it : it + 1, :] = ab[0:1, 0:probes]
        betas_ref[it : it + 1, :] = ab[1:2, 0:probes]
    scale = 1.0 / beta
    for c in range(WB):
        q = (block_of(win_ref, c, 0, probes) - alpha * block_of(old_ref, c, 0, probes)) * scale
        if c // HB in (1, 2, 3):
            part = c // HB + half - 2

            @pl.when((part >= 0) & (part < 2))
            def _(q=q, part=part, c=c):
                at = pl.multiple_of((part * HB + c % HB) * BL, BL)
                last_ref[:, pl.ds(at, BL)] = q

        high, low = split(q)
        sign = block_of(first_ref, c, 0, probes).astype(BF16)
        left_of[c] = jnp.concatenate([high, low, sign, sign], axis=0).T
        if c // HB == 2:
            right_of[c % HB] = jnp.concatenate([sign, sign, high, low], axis=0)
    acc[...] = jnp.zeros_like(acc)

    def step(u, _):
        made = []
        for t in range(2):
            i = 2 * u + t
            a = ap_ref[i]
            right = right_of[a]
            made.append(
                [
                    jnp.dot(left_of[wb_ref[2 * i + e]], right, preferred_element_type=F32)
                    for e in range(2)
                ]
            )
        for t in range(2):
            i = 2 * u + t
            a = ap_ref[i]
            sums = [None] * 3
            for e in range(2):
                c = wb_ref[2 * i + e]
                weight = made[t][e] * dbuf[i, pl.ds(e * BL, BL), :]
                for k in range(3):
                    term = weight * (xb[c, k] - own_row(x_ref, half, a, k))
                    term = jnp.sum(term.reshape(16, 8, BL), axis=0)
                    sums[k] = term if sums[k] is None else sums[k] + term
            for k in range(3):
                acc[a, k] += sums[k]
        return 0

    lax.fori_loop(0, np_ref[0] // 2, step, 0)
    g_ref[...] = jnp.zeros_like(g_ref)
    for a in range(HB):
        for k in range(3):
            g_ref[k : k + 1, a * BL : (a + 1) * BL] = jnp.sum(acc[a, k], axis=0, keepdims=True)


def grad(lists, slopes, window, old, stats, first, points, spread, ab0, ab1, total_pts):
    probes = window.shape[1]
    return pl.pallas_call(
        functools.partial(grad_kernel, total_pts),
        out_shape=(
            sds((probes, 2 * HB * BL)),
            sds((ITERS, probes)),
            sds((ITERS, probes)),
            sds((8, HB * BL)),
        ),
        in_specs=[SMEM, SMEM, SMEM] + [VMEM] * 9,
        out_specs=(VMEM,) * 4,
        scratch_shapes=[
            pltpu.VMEM((8, BL), F32),
            pltpu.VMEM((WB, BL, 4 * probes), BF16),
            pltpu.VMEM((HB, 4 * probes, BL), BF16),
            pltpu.VMEM((HB, 3, 8, BL), F32),
        ],
        compiler_params=pltpu.CompilerParams(vmem_limit_bytes=GRAD_VMEM),
        name="grad",
    )(*lists, slopes, window, old, stats, first, points, spread, ab0, ab1)


def multiplicity(rows, cols, tots, half, slots):
    spot = jnp.arange(slots, dtype=jnp.int32)[None, :]
    frame = jnp.array([0, 0, SB, SB], jnp.int32)[:, None]
    rows = rows.reshape(4, slots)
    offs = cols.reshape(4, slots) - rows
    live = spot < tots.reshape(4, 1)
    key = jnp.where(live, (rows + frame) * 32 + offs, -1).reshape(-1)
    out = SB + HB * half + jnp.arange(HB, dtype=jnp.int32)[:, None]
    off = jnp.arange(-SB, SB + 1, dtype=jnp.int32)[None, :]
    ahead = jnp.where(off >= 0, out * 32 + off, -2).reshape(-1)
    behind = jnp.where(off <= 0, (out + off) * 32 - off, -2).reshape(-1)
    hits = (ahead[:, None] == key).astype(jnp.int32) + (behind[:, None] == key)
    return jnp.sum(hits, axis=1)


def body(coords, noise_var, probe_signs, tile_rows, tile_cols, tile_count):
    half = lax.axis_index("sub")
    blk = lax.axis_size("blk")
    slab_pts = coords.shape[1]
    half_pts = slab_pts // 2
    probes = probe_signs.shape[0]
    total_pts = slab_pts * blk
    all_probes = probes * lax.axis_size("probe")
    slots = tile_rows.size
    signs = lax.dynamic_slice_in_dim(probe_signs, half * half_pts, half_pts, 1)
    pair = ("blk", "sub")
    every = [(b, h) for b in range(blk) for h in range(2)]

    def hop(step, flip):
        perm = [(2 * b + h, (b + step(h)) % blk * 2 + (1 - h if flip else h)) for b, h in every]
        return lax.ppermute(signs, pair, perm)

    below, above, cross = hop(lambda h: 1, 0), hop(lambda h: -1, 0), hop(lambda h: 2 * h - 1, 1)
    points, *lists = entry(coords, tile_rows.reshape(1, -1), tile_cols.reshape(1, -1), tile_count)
    noise = noise_var.reshape(1, -1)
    *index, tiles, slopes, spread, points = build(multiplicity(*lists, half, slots), points)
    work, stat, first = first_apply(index, tiles, slopes, probe_signs, below, above, cross, noise)
    old = first
    pairs = []
    for it in range(1, ITERS):
        window, stats = exchange(work, stat, it)
        work, stat, old, ab = apply(index, tiles, slopes, window, old, stats, noise, total_pts)
        pairs.append(ab)
    window, stats = exchange(work, stat, ITERS)
    last, alphas, betas, part = grad(
        index, slopes, window, old, stats, first, points, spread, *pairs, total_pts
    )
    parts = share(part, ITERS + 1)
    parts = jnp.sum(parts.reshape(-1, 2, 8, half_pts), axis=0)[:, 0:3]
    warp = jnp.tanh(coords)
    factor = (SCALE * 2.0 / (TAPER_SQ * all_probes)) * (1.0 + WARP_GAIN * (1.0 - warp * warp))
    coord_grad = factor * jnp.concatenate([parts[0], parts[1]], axis=1)
    return (alphas, betas, last, coord_grad)


def solution(mesh):
    return jax.shard_map(
        body,
        mesh=mesh,
        in_specs=(
            P(None, ("groups", "blk")),
            P(("groups", "blk")),
            P("probe", ("groups", "blk")),
            P(("groups", "blk"), "sub", None),
            P(("groups", "blk"), "sub", None),
            P(("groups", "blk"), "sub"),
        ),
        out_specs=(
            P(None, ("groups", "probe")),
            P(None, ("groups", "probe")),
            P("probe", ("groups", "blk")),
            P(None, ("groups", "blk")),
        ),
        check_vma=False,
    )
```

```python
import functools
import math

import jax
import jax.numpy as jnp
from jax import lax
from jax.experimental import pallas as pl
from jax.experimental.pallas import tpu as pltpu
from jax.sharding import PartitionSpec as P

ITERS = 3
SIGNAL_VAR = 0.1
LENGTH_SQ = 2.0
TAPER_SQ = 16.0
WARP_GAIN = 0.4
EPSILON = 1e-06

F32 = jnp.float32
BF16 = jnp.bfloat16
BL = 128
SB = 16
HB = 8
WB = 5 * HB
OFFS = 2 * SB + 1
SLOTS = 272
ZERO = SLOTS - 1
TINY = 1e-30
SCALE = math.sqrt(TAPER_SQ)
EXPO = -TAPER_SQ / (2.0 * LENGTH_SQ) / math.log(2.0)
SLOPE = TAPER_SQ / (2.0 * LENGTH_SQ)
BUILD_VMEM = 2**22
APPLY_VMEM = 8 * 2**20
GRAD_VMEM = 6 * 2**20
VMEM = pl.BlockSpec(memory_space=pltpu.VMEM)
SMEM = pl.BlockSpec(memory_space=pltpu.SMEM)
HBM = pl.BlockSpec(memory_space=pltpu.HBM)
MESH = pl.DeviceIdType.MESH


def sds(shape, dtype=F32):
    return jax.ShapeDtypeStruct(shape, dtype)


def peer_of(me, step, n, axis):
    to = lax.rem(me + step + n, n)
    return {axis: to // 2, "sub": lax.rem(to, 2)}


def greet(peers):
    barrier = pltpu.get_barrier_semaphore()
    for peer in peers:
        pl.semaphore_signal(barrier, inc=1, device_id=peer, device_id_type=MESH)
    return barrier


def remote(src, dst, send, recv, peer):
    return pltpu.make_async_remote_copy(
        src_ref=src, dst_ref=dst, send_sem=send, recv_sem=recv,
        device_id=peer, device_id_type=MESH,
    )


def ship(src, win_ref, sems, up, down, twin, direct):
    wsend, wrecv, fsend, frecv = sems
    half = lax.axis_index("sub")
    chunks = src.shape[0] // 8
    rows = [pl.ds(8 * c, 8) for c in range(chunks)]
    outs = []
    for c in range(chunks):
        outs.append(remote(src.at[rows[c]], win_ref.at[0, rows[c]], wsend.at[0, c], wrecv.at[0, c], up))
        outs.append(remote(src.at[rows[c]], win_ref.at[4, rows[c]], wsend.at[1, c], wrecv.at[1, c], down))
    for copy in outs:
        copy.start()
    own = None
    if direct:
        own = remote(src, win_ref.at[1 + 2 * half], fsend.at[chunks], frecv.at[chunks], twin)
        own.start()

    def hand(c):
        piece = win_ref.at[4 - 4 * half, rows[c]]
        return piece, remote(piece, win_ref.at[3 - 2 * half, rows[c]], fsend.at[c], frecv.at[c], twin)

    def wait_twin():
        if direct:
            own.wait()

    def forward():
        for c in range(chunks):
            piece, copy = hand(c)
            remote(piece, piece, wsend.at[0, c], wrecv.at[1 - half, c], twin).wait_recv()
            copy.start()

    def wait_direct():
        for c in range(chunks):
            other = win_ref.at[4 * half, rows[c]]
            remote(other, other, wsend.at[0, c], wrecv.at[half, c], twin).wait_recv()

    def wait_handed():
        for c in range(chunks):
            hand(c)[1].wait_recv()

    def drain():
        for copy in outs:
            copy.wait_send()
        for c in range(chunks):
            hand(c)[1].wait_send()

    return wait_twin, forward, wait_direct, wait_handed, drain


def ship_sems(chunks):
    dma = pltpu.SemaphoreType.DMA
    return [dma((2, chunks)), dma((2, chunks)), dma((chunks + 1,)), dma((chunks + 1,))]


def entry_kernel(n, x_ref, l_ref, win_ref, lists_ref, send, recv, lsem):
    blk, half = lax.axis_index("blk"), lax.axis_index("sub")
    above, below = lax.rem(blk + 1, n), lax.rem(blk + n - 1, n)
    up = {"blk": above, "sub": half}
    down = {"blk": below, "sub": half}
    cross = {"blk": above, "sub": 1 - half}
    under = {"blk": below, "sub": 1 - half}
    twin = {"blk": blk, "sub": 1 - half}
    barrier = greet((up, down, cross, under, twin))
    local = [
        pltpu.make_async_copy(x_ref, win_ref.at[1], lsem.at[0]),
        pltpu.make_async_copy(l_ref, lists_ref.at[2], lsem.at[1]),
    ]
    for copy in local:
        copy.start()
    pl.semaphore_wait(barrier, 5)
    copies = [
        remote(x_ref, win_ref.at[0], send.at[0], recv.at[0], up),
        remote(x_ref, win_ref.at[2], send.at[1], recv.at[1], down),
        remote(l_ref, lists_ref.at[1], send.at[2], recv.at[2], cross),
        remote(l_ref, lists_ref.at[0], send.at[3], recv.at[3], up),
        remote(l_ref, lists_ref.at[3], send.at[4], recv.at[4], twin),
    ]
    for copy in copies:
        copy.start()
    for copy in local:
        copy.wait()
    for copy in copies:
        copy.wait()


def entry(coords, listed):
    dma = pltpu.SemaphoreType.DMA
    return pl.pallas_call(
        functools.partial(entry_kernel, lax.axis_size("blk")),
        out_shape=(sds((3,) + coords.shape), sds((4,) + listed.shape, jnp.int32)),
        in_specs=[VMEM] * 2,
        out_specs=(VMEM,) * 2,
        scratch_shapes=[dma((5,)), dma((5,)), dma((2,))],
        compiler_params=pltpu.CompilerParams(
            collective_id=0, has_side_effects=True, vmem_limit_bytes=2**21
        ),
        name="entry",
    )(coords, listed)


def share_kernel(n, own_ref, all_ref, send, recv, lsem):
    me = lax.axis_index("probe") * 2 + lax.axis_index("sub")

    def device(step):
        to = lax.rem(me + step, n)
        return {"probe": to // 2, "sub": lax.rem(to, 2)}

    barrier = pltpu.get_barrier_semaphore()
    for step in range(1, n):
        pl.semaphore_signal(barrier, inc=1, device_id=device(step), device_id_type=MESH)
    local = pltpu.make_async_copy(own_ref, all_ref.at[me], lsem)
    local.start()
    pl.semaphore_wait(barrier, n - 1)
    copies = []
    for step in range(1, n):
        copies.append(
            pltpu.make_async_remote_copy(
                src_ref=own_ref,
                dst_ref=all_ref.at[me],
                send_sem=send.at[step],
                recv_sem=recv.at[step],
                device_id=device(step),
                device_id_type=MESH,
            )
        )
    for copy in copies:
        copy.start()
    local.wait()
    for copy in copies:
        copy.wait()


def share(own, ident):
    n = lax.axis_size("probe") * 2
    return pl.pallas_call(
        functools.partial(share_kernel, n),
        out_shape=sds((n,) + own.shape),
        in_specs=[VMEM],
        out_specs=VMEM,
        scratch_shapes=[
            pltpu.SemaphoreType.DMA((n,)),
            pltpu.SemaphoreType.DMA((n,)),
            pltpu.SemaphoreType.DMA,
        ],
        compiler_params=pltpu.CompilerParams(collective_id=ident, has_side_effects=True, vmem_limit_bytes=2**21),
        name="share",
    )(own)


def block_of(ref, block, lo, hi):
    return ref[block // HB, lo:hi, (block % HB) * BL : (block % HB + 1) * BL]


def spread_points(x_ref, xb, half):
    for c in range(WB):
        at = c + HB * half
        flat = x_ref[at // SB, :, pl.ds(pl.multiple_of((at % SB) * BL, BL), BL)]
        cols = jnp.concatenate([flat, flat, flat[0:2]], axis=0).T
        for k in range(3):
            xb[c, k] = jnp.broadcast_to(cols[:, k : k + 1], (BL, BL))


def own_row(x_ref, half, a, k):
    return x_ref[1, k : k + 1, pl.ds(pl.multiple_of((a + HB * half) * BL, BL), BL)]


def local_stats(q, w, st_ref):
    square = jnp.sum(q * q, axis=1, keepdims=True)
    guess = jnp.sum(q * w, axis=1, keepdims=True) / jnp.maximum(square, TINY)
    rest = w - guess * q
    resid = jnp.sum(rest * rest, axis=1, keepdims=True)
    lane = lax.broadcasted_iota(jnp.int32, (q.shape[0], BL), 1)
    mixed = jnp.where(lane == 0, guess, jnp.where(lane == 1, resid, square))
    full = jnp.concatenate([mixed] * (BL // q.shape[0]), axis=0)
    st_ref[...] = full.T[0:8, :]


def alpha_beta(st_ref, ab_ref, n, probes, total_pts):
    guess = [st_ref[d, 0:1, :] for d in range(n)]
    square = [st_ref[d, 2:3, :] for d in range(n)]
    alpha = guess[0] * square[0]
    for d in range(1, n):
        alpha = alpha + guess[d] * square[d]
    alpha = alpha / total_pts
    resid = jnp.zeros_like(alpha)
    for d in range(n):
        gap = alpha - guess[d]
        resid = resid + (st_ref[d, 1:2, :] + gap * gap * square[d])
    beta = jnp.sqrt(resid / total_pts + EPSILON)
    row = lax.broadcasted_iota(jnp.int32, (8, BL), 0)
    ab = jnp.where(row == 0, alpha, beta)
    ab_ref[...] = ab
    cols = jnp.concatenate([ab] * 16, axis=0).T
    return cols[0:probes, 0:1], cols[0:probes, 1:2]


def split(value):
    high = value.astype(BF16)
    return high, (value - high.astype(F32)).astype(BF16)


def multiplicity(lists_ref, slots, half):
    out = lax.broadcasted_iota(jnp.int32, (HB, BL), 0) + (SB + HB * half)
    off = lax.broadcasted_iota(jnp.int32, (BL, BL), 0) - SB
    spot = lax.broadcasted_iota(jnp.int32, (1, BL), 1)
    total = jnp.zeros((HB, BL), F32)
    for k in range(4):
        row = lists_ref[k, 0:1]
        step = lists_ref[k, 1:2] - row
        row = jnp.where(spot < lists_ref[k, 0:1, slots : slots + 1], row + (0 if k < 2 else SB), -4 * SB)
        for block, gap in ((row, step), (row + step, -step)):
            here = jnp.where(out == block, 1.0, 0.0).astype(BF16)
            there = jnp.where(off == gap, 1.0, 0.0).astype(BF16)
            total = total + lax.dot_general(
                here, there, (((1,), (1,)), ((), ())), preferred_element_type=F32
            )
    return total.astype(jnp.int32)


def build_kernel(
    slots, raw_ref, lists_ref, tab_ref, code_ref, np_ref, k_ref, dbuf, xb, x_ref,
    mv, ms, sem,
):
    half = lax.axis_index("sub")
    mv[...] = multiplicity(lists_ref, slots, half)
    move = pltpu.make_async_copy(mv, ms, sem)
    move.start()
    for slab in range(3):
        raw = raw_ref[slab]
        x_ref[slab] = (raw + WARP_GAIN * jnp.tanh(raw)) * (1.0 / SCALE)
    spread_points(x_ref, xb, half)
    k_ref[ZERO] = jnp.zeros((BL, 2 * BL), BF16)
    for a in range(HB):
        for w in list(range(a)) + list(range(a + OFFS, WB)):
            tab_ref[a * WB + w] = ZERO
    move.wait()

    def fill(a, at):
        for o in range(OFFS):
            live = (ms[a, o] > 0).astype(jnp.int32)
            code_ref[at] = a * 64 + o
            tab_ref[a * WB + a + o] = ZERO + live * (at - ZERO)
            at = at + live
        return at

    used = lax.fori_loop(0, HB, fill, 0)
    for t in range(4):
        code_ref[used + t] = SB
    padded = (used + 3) // 4 * 4
    np_ref[0] = padded

    def step(u, _):
        for e in range(2):
            i = 2 * u + e
            code = code_ref[i]
            a, o = code // 64, lax.rem(code, 64)
            times = (ms[a, o] * (i < used).astype(jnp.int32)).astype(F32) * SIGNAL_VAR
            dist = None
            for k in range(3):
                differ = xb[a + o, k] - own_row(x_ref, half, a, k)
                dist = differ * differ if dist is None else dist + differ * differ
            taper = jnp.maximum(1.0 - dist, 0.0)
            weight = times * jnp.exp2(dist * EXPO) * taper
            high, low = split(weight * taper)
            k_ref[i, :, 0:BL] = high
            k_ref[i, :, BL : 2 * BL] = low
            dbuf[i] = weight * (taper * SLOPE + 2.0)
        return 0

    lax.fori_loop(0, padded // 2, step, 0)


def build(points, lists, slots):
    return pl.pallas_call(
        functools.partial(build_kernel, slots),
        out_shape=(
            sds((HB * WB,), jnp.int32),
            sds((SLOTS,), jnp.int32),
            sds((1,), jnp.int32),
            pltpu.VMEM((SLOTS, BL, 2 * BL), BF16),
            pltpu.VMEM((SLOTS, BL, BL), F32),
            pltpu.VMEM((WB, 3, BL, BL), F32),
            sds(points.shape),
        ),
        in_specs=[VMEM] * 2,
        out_specs=(SMEM, SMEM, SMEM, VMEM, VMEM, VMEM, VMEM),
        scratch_shapes=[
            pltpu.VMEM((HB, BL), jnp.int32),
            pltpu.SMEM((HB, BL), jnp.int32),
            pltpu.SemaphoreType.DMA,
        ],
        compiler_params=pltpu.CompilerParams(vmem_limit_bytes=BUILD_VMEM),
        cost_estimate=pl.CostEstimate(flops=10**9, bytes_accessed=10**7, transcendentals=10**7),
        name="build",
    )(points, lists)


def noise_row(noise_ref, a):
    at = (a + HB * lax.axis_index("sub")) * BL
    return noise_ref[0:1, pl.ds(pl.multiple_of(at, BL), BL)]


def lanczos_kernel(
    n, total_pts, tab_ref, k_ref, slopes_ref, signs_ref, noise_ref,
    q_ref, first_ref, *refs,
):
    abs_ref, refs = refs[:ITERS], refs[ITERS:]
    sv, win, work, image, st, all_ref, vb, acc, lsem, ssend, srecv, *wsems = refs
    probes = first_ref.shape[1]
    blk, half = lax.axis_index("blk"), lax.axis_index("sub")
    me = blk * 2 + half
    twin = {"blk": blk, "sub": 1 - half}
    up, down = peer_of(me, 2, n, "blk"), peer_of(me, -2, n, "blk")
    pairs, handed, direct, passed = 3 - 2 * half, 1 + 2 * half, 4 * half, 4 - 4 * half
    pass_late = (half == 1) & (blk == 0) | (half == 0) & (blk == n // 2 - 1)
    barrier = greet([peer_of(me, step, n, "blk") for step in range(1, n)])
    wide = HB * BL

    def lanes(side):
        return pl.ds(pl.multiple_of(side * wide, wide), wide)

    mine = signs_ref.at[:, lanes(half)]
    local = [
        pltpu.make_async_copy(mine, sv.at[2], lsem.at[0]),
        pltpu.make_async_copy(signs_ref.at[:, lanes(1 - half)], sv.at[pairs], lsem.at[1]),
    ]
    for copy in local:
        copy.start()
    pl.semaphore_wait(barrier, n - 1)

    def part_product(p, rows):
        def step(u, _):
            made = []
            for t in range(2):
                at = (2 * u + t) * WB + p * HB
                right = jnp.concatenate([k_ref[tab_ref[at + w]] for w in range(HB)], axis=0)
                both = jnp.dot(vb[p, 0:rows], right, preferred_element_type=F32)
                both = both[:, 0:BL] + both[:, BL : 2 * BL]
                made.append(both if rows == probes else both[0:probes] + both[probes:])
            for t in range(2):
                acc[2 * u + t] += made[t]
            return 0

        lax.fori_loop(0, HB // 2, step, 0)

    def sweep(waits, load, rows):
        wait_twin, forward, wait_direct, wait_handed, drain = waits

        def part(p):
            load(p)
            part_product(p, rows)

        acc[...] = jnp.zeros_like(acc)
        part(2)
        wait_twin()
        part(pairs)

        @pl.when(jnp.logical_not(pass_late))
        def _():
            forward()
            part(passed)
            wait_direct()
            part(direct)
            wait_handed()
            part(handed)

        @pl.when(pass_late)
        def _():
            wait_direct()
            part(direct)
            wait_handed()
            part(handed)
            forward()
            part(passed)

        drain()

    def finish(it, beta):
        for a in range(HB):
            at = slice(a * BL, (a + 1) * BL)
            value = image[:, at] + noise_row(noise_ref, a) * q_ref[2, :, at]
            if it > 0:
                value = value - beta * work[ITERS, :, at]
            work[it, :, at] = value
        local_stats(q_ref[2], work[it], st.at[it])
        all_ref[it, me] = st[it]
        stats = [
            remote(st.at[it], all_ref.at[it, me], ssend.at[it, step], srecv.at[it, step], peer_of(me, step, n, "blk"))
            for step in range(1, n)
        ]
        for copy in stats:
            copy.start()
        waits = ship(work.at[it], win.at[it], wsems[4 + 4 * it : 8 + 4 * it], up, down, twin, True)
        return waits, stats

    def advance(it, stats):
        for copy in stats:
            copy.wait()
        return alpha_beta(all_ref.at[it], abs_ref[it], n, probes, total_pts)

    def window(it, p):
        return work[it] if p is None else win[it, p]

    waits = ship(mine, sv, wsems[0:4], up, down, twin, False)
    for copy in local:
        copy.wait()

    def load_signs(p):
        value = sv[p].astype(F32)
        first_ref[p] = value
        q_ref[p] = value
        vb[p, 0:probes] = value.astype(BF16)

    sweep(waits, load_signs, probes)
    for a in range(HB):
        image[:, a * BL : (a + 1) * BL] = acc[a]
    waits, stats = finish(0, None)
    for it in range(ITERS):
        win[it, 2] = work[it]
        if it < ITERS - 1:

            def load(p, it=it):
                high, low = split(win[it, p])
                vb[p, 0:probes] = high
                vb[p, probes : 2 * probes] = low

            sweep(waits, load, 2 * probes)
        else:
            wait_twin, forward, wait_direct, wait_handed, drain = waits
            wait_twin()
            forward()
            wait_direct()
            wait_handed()
            drain()
        alpha, beta = advance(it, stats)
        scale = 1.0 / beta
        work[ITERS] = q_ref[2]
        for p in range(5):
            q_ref[p] = (win[it, p] - alpha * q_ref[p]) * scale
        if it < ITERS - 1:
            for a in range(HB):
                at = slice(a * BL, (a + 1) * BL)
                image[:, at] = (acc[a] - alpha * image[:, at]) * scale
            waits, stats = finish(it + 1, beta)


def lanczos(tab, tiles, slopes, signs, noise, total_pts):
    probes = signs.shape[0]
    n = lax.axis_size("blk") * 2
    wide = HB * BL
    dma = pltpu.SemaphoreType.DMA
    sems = [sem for _ in range(ITERS + 1) for sem in ship_sems(probes // 8)]
    return pl.pallas_call(
        functools.partial(lanczos_kernel, n, total_pts),
        out_shape=(sds((5, probes, wide)),) * 2 + (sds((8, BL)),) * ITERS,
        in_specs=[SMEM, VMEM, VMEM, HBM, VMEM],
        out_specs=(VMEM,) * (2 + ITERS),
        scratch_shapes=[
            pltpu.VMEM((5, probes, wide), jnp.int32),
            pltpu.VMEM((ITERS, 5, probes, wide), F32),
            pltpu.VMEM((ITERS + 1, probes, wide), F32),
            pltpu.VMEM((probes, wide), F32),
            pltpu.VMEM((ITERS, 8, BL), F32),
            pltpu.VMEM((ITERS, n, 8, BL), F32),
            pltpu.VMEM((5, 2 * probes, wide), BF16),
            pltpu.VMEM((HB, probes, BL), F32),
            dma((2,)),
            dma((ITERS, n)),
            dma((ITERS, n)),
        ] + sems,
        compiler_params=pltpu.CompilerParams(
            collective_id=1, has_side_effects=True, vmem_limit_bytes=APPLY_VMEM
        ),
        name="lanczos",
    )(tab, tiles, slopes, signs, noise)


def grad_kernel(
    code_ref, np_ref, dbuf, win_ref, first_ref, x_ref, xb, ab0, ab1, ab2,
    last_ref, alphas_ref, betas_ref, g_ref, left_of, right_of, acc,
):
    half = lax.axis_index("sub")
    probes = win_ref.shape[1]
    for it, ab in enumerate((ab0, ab1, ab2)):
        alphas_ref[it : it + 1, :] = ab[0:1, 0:probes]
        betas_ref[it : it + 1, :] = ab[1:2, 0:probes]
    wide = HB * BL
    for side in range(2):
        last_ref[:, side * wide : (side + 1) * wide] = win_ref[2 + side - half]
    for c in range(WB):
        high, low = split(block_of(win_ref, c, 0, probes))
        sign = block_of(first_ref, c, 0, probes).astype(BF16)
        left_of[c] = jnp.concatenate([high, low, sign, sign], axis=0).T
        if c // HB == 2:
            right_of[c % HB] = jnp.concatenate([sign, sign, high, low], axis=0)
    acc[...] = jnp.zeros_like(acc)

    def step(u, _):
        codes = [code_ref[4 * u + t] for t in range(4)]
        rows = [code // 64 for code in codes]
        cols = [code // 64 + lax.rem(code, 64) for code in codes]
        made = [
            jnp.dot(left_of[c], right_of[a], preferred_element_type=F32) for a, c in zip(rows, cols)
        ]
        for t in range(4):
            a, c = rows[t], cols[t]
            weight = made[t] * dbuf[4 * u + t]
            for k in range(3):
                term = weight * (xb[c, k] - own_row(x_ref, half, a, k))
                acc[a, k] += jnp.sum(term.reshape(16, 8, BL), axis=0)
        return 0

    lax.fori_loop(0, np_ref[0] // 4, step, 0)
    g_ref[...] = jnp.zeros_like(g_ref)
    for a in range(HB):
        for k in range(3):
            g_ref[k : k + 1, a * BL : (a + 1) * BL] = jnp.sum(acc[a, k], axis=0, keepdims=True)


def grad(code, count, slopes, window, first, points, spread, pairs):
    probes = window.shape[1]
    return pl.pallas_call(
        grad_kernel,
        out_shape=(
            sds((probes, 2 * HB * BL)),
            sds((ITERS, probes)),
            sds((ITERS, probes)),
            sds((8, HB * BL)),
        ),
        in_specs=[SMEM, SMEM] + [VMEM] * 8,
        out_specs=(VMEM,) * 4,
        scratch_shapes=[
            pltpu.VMEM((WB, BL, 4 * probes), BF16),
            pltpu.VMEM((HB, 4 * probes, BL), BF16),
            pltpu.VMEM((HB, 3, 8, BL), F32),
        ],
        compiler_params=pltpu.CompilerParams(vmem_limit_bytes=GRAD_VMEM),
        name="grad",
    )(code, count, slopes, window, first, points, spread, *pairs)


def body(coords, noise_var, probe_signs, tile_rows, tile_cols, tile_count):
    blk = lax.axis_size("blk")
    slab_pts = coords.shape[1]
    half_pts = slab_pts // 2
    probes = probe_signs.shape[0]
    total_pts = slab_pts * blk
    all_probes = probes * lax.axis_size("probe")
    slots = tile_rows.size
    tail = jnp.broadcast_to(tile_count.reshape(1, 1), (1, BL - slots))
    listed = jnp.concatenate(
        [tile_rows.reshape(1, -1), tail, tile_cols.reshape(1, -1), tail], axis=1
    ).reshape(2, BL)
    points, lists = entry(coords, listed)
    noise = noise_var.reshape(1, -1)
    tab, code, count, tiles, slopes, spread, points = build(points, lists, slots)
    window, first, *pairs = lanczos(tab, tiles, slopes, probe_signs, noise, total_pts)
    last, alphas, betas, part = grad(code, count, slopes, window, first, points, spread, pairs)
    parts = share(part, 2)
    parts = jnp.sum(parts.reshape(-1, 2, 8, half_pts), axis=0)[:, 0:3]
    warp = jnp.tanh(coords)
    factor = (SCALE * 2.0 / (TAPER_SQ * all_probes)) * (1.0 + WARP_GAIN * (1.0 - warp * warp))
    coord_grad = factor * jnp.concatenate([parts[0], parts[1]], axis=1)
    return (alphas, betas, last, coord_grad)


def solution(mesh):
    return jax.shard_map(
        body,
        mesh=mesh,
        in_specs=(
            P(None, ("groups", "blk")),
            P(("groups", "blk")),
            P("probe", ("groups", "blk")),
            P(("groups", "blk"), "sub", None),
            P(("groups", "blk"), "sub", None),
            P(("groups", "blk"), "sub"),
        ),
        out_specs=(
            P(None, ("groups", "probe")),
            P(None, ("groups", "probe")),
            P("probe", ("groups", "blk")),
            P(None, ("groups", "blk")),
        ),
        check_vma=False,
    )
```
